128 devices in a mesh: cluster: 4 (over z), sub: 32 (over y, x, core).
Axes of the slice: x: 4, y: 4, z: 4, core: 2. Of those that a mesh axis runs over, the one named last changes fastest.
Arguments:
- dual_operators: bfloat16 [256, 2048, 2048], P(('cluster', 'sub')), may hold values from -1 to 3, as said below
- local_loads: float32 [256, 2048, 128], P(('cluster', 'sub')), may hold values from -15 to 15
- modes: float32 [256, 6, 2048], P(('cluster', 'sub')), may hold values from -4 to 4
- coarse_matrix: float32 [1536, 1536], P(('cluster', 'sub')), may hold values from -1 to 1, as said below
- coarse_loads: float32 [1536, 128], replicated, may hold values from -6144 to 6144
- slot_block: int32 [128, 32], P(('cluster', 'sub')), may hold values from 0 to 31, each once within a row
Outputs:
- multipliers: float32 [256, 2048, 128], P(('cluster', 'sub'))
- projected_residual: float32 [256, 2048, 128], P(('cluster', 'sub'))
The draws below stay inside these ranges and needn't reach their ends.
Inputs may be any that keep to these rules, and one draw needn't show every extreme that they name: `dual_operators`: each subdomain's matrix is symmetric and positive definite. `coarse_matrix`: Symmetric.
All inputs are finite; a program needn't handle non-finite values.
Results may differ from the reference program's by a relative error of at most 0.0018.
Values sent between devices are 32-bit elements; how exact they have to be, the bound alone decides.
No kernel may reach another device: no remote copies, remote signals or barrier semaphores. Data moves between devices by JAX's collectives and lax.ppermute only.
A program may use at most 128 MiB of HBM per device.

```python
import math
import jax
import jax.numpy as jnp
from jax import lax

M = 2048
BLK = 128
NMODE = 6
LOADS = 128
ITERS = 3
NBD = 32
N_SUBDOM = 256
NC = 1536
N_CLUSTER = 4
N_SUB = 32
DEVICES = 128


def symmetric_noise(noise_key, order):
    noise = jnp.clip(jax.random.normal(noise_key, (order, order), jnp.float32), -5.0, 5.0)
    return (noise + noise.T) / math.sqrt(2.0)


def draw_dual_operators(key, part):

    def one_matrix(index):
        noise_key, diag_key = jax.random.split(jax.random.fold_in(key, index))
        symmetric = symmetric_noise(noise_key, M) * (0.45 / math.sqrt(M))
        diagonal = jax.random.uniform(diag_key, (M,), jnp.float32, 1.0, 3.0)
        row_ids = lax.broadcasted_iota(jnp.int32, (M, M), 0)
        col_ids = lax.broadcasted_iota(jnp.int32, (M, M), 1)
        return jnp.where(row_ids == col_ids, diagonal[:, None], symmetric).astype(jnp.bfloat16)
    return lax.map(one_matrix, jnp.arange(N_SUBDOM, dtype=jnp.int32))


def draw_coarse_matrix(key, part):
    noise_key, diag_key = jax.random.split(jax.random.fold_in(key, 7))
    symmetric = symmetric_noise(noise_key, NC) * (0.5 / math.sqrt(NC) / M)
    diagonal = jnp.exp(jax.random.uniform(diag_key, (NC,), jnp.float32, math.log(0.5), math.log(2.0))) / M
    row_ids = lax.broadcasted_iota(jnp.int32, (NC, NC), 0)
    col_ids = lax.broadcasted_iota(jnp.int32, (NC, NC), 1)
    return jnp.where(row_ids == col_ids, diagonal[:, None], symmetric).astype(jnp.float32)


def draw_local_loads(key, part):
    noise_key = jax.random.fold_in(key, 11)
    noise = jnp.clip(jax.random.normal(noise_key, (N_SUBDOM, M, LOADS), jnp.float32), -5.0, 5.0)
    rising = 1.0 + 2.0 * jnp.arange(N_SUBDOM, dtype=jnp.float32) / (N_SUBDOM - 1)
    return (noise * rising[:, None, None]).astype(jnp.float32)


def level_of(stream_key, shape, pieces, low, largest):
    factor_of, own = 1.0, jax.random.fold_in(stream_key, 6)
    for axis_at, shards_of in pieces:
        draws = jnp.exp(jax.random.uniform(jax.random.fold_in(own, axis_at), (shards_of,), jnp.float32, low / len(pieces), largest / len(pieces)))
        factor_of = factor_of * jnp.repeat(draws, shape[axis_at] // shards_of).reshape([-1 if axis == axis_at else 1 for axis in range(len(shape))])
    return factor_of


def bell_draw(own_key, shape, spread, bound, pieces=(), kind=jnp.bfloat16):
    result = jax.random.normal(own_key, shape, jnp.float32) * spread
    if len(pieces) > 0:
        result = level_of(own_key, shape, pieces, -0.22, 0.18) * result
    return jnp.clip(result, min=-bound, max=bound).astype(kind)


def setup_inputs(seed: int = 0) -> dict:
    streams_of = jax.random.split(jax.random.key(seed), 7)
    dual_operators = draw_dual_operators(jax.random.fold_in(streams_of[6], 71), 0)
    local_loads = draw_local_loads(jax.random.fold_in(streams_of[6], 71), 0)
    modes = bell_draw(streams_of[2], (N_SUBDOM, NMODE, M), 1.0, 4.0, ((0, 128),), jnp.float32)
    coarse_matrix = draw_coarse_matrix(jax.random.fold_in(streams_of[6], 71), 0)
    coarse_loads = bell_draw(streams_of[4], (NC, LOADS), (0.5 * M), 6144.0, (), jnp.float32)
    slot_block = jax.vmap(lambda own: jax.random.permutation(own, NBD))(jax.random.split(streams_of[5], DEVICES)).reshape((DEVICES, NBD)).astype(jnp.int32)
    return {"dual_operators": dual_operators, "local_loads": local_loads, "modes": modes, "coarse_matrix": coarse_matrix, "coarse_loads": coarse_loads, "slot_block": slot_block}


def reference(dual_operators, local_loads, modes, coarse_matrix, coarse_loads, slot_block):
    highest = lax.Precision.HIGHEST
    device_total = N_CLUSTER * N_SUB
    block_total = slot_block.shape[1]
    face_size = block_total // 8
    positions = jnp.arange(block_total, dtype=jnp.int32)
    inverse = jnp.sum(positions[None, :, None] * (slot_block[:, :, None] == positions[None, None, :]).astype(jnp.int32), axis=1).astype(jnp.int32)
    device_ids = jnp.arange(device_total, dtype=jnp.int32)
    cluster_ids = (device_ids // N_SUB)[:, None]
    sub_ids = (device_ids % N_SUB)[:, None]
    face_ids = (positions // face_size)[None, :]
    shared = ((face_ids == 0) & (sub_ids > 0)) | ((face_ids == 1) & (sub_ids < N_SUB - 1)) | ((face_ids == 2) & (cluster_ids > 0)) | ((face_ids == 3) & (cluster_ids < N_CLUSTER - 1)) | (face_ids >= 6)
    slot_weights = jnp.where(shared, 0.5, 1.0).astype(jnp.float32)
    weights = jnp.repeat(jnp.take_along_axis(slot_weights, inverse, axis=1), BLK, axis=1).reshape(N_SUBDOM, M)

    def receive(slot_grid):
        def face_slots(index):
            return slot_grid[:, :, index * face_size:(index + 1) * face_size]

        blank_faces = jnp.zeros_like(face_slots(0))
        lower_sub = jnp.concatenate([blank_faces[:, :1], face_slots(1)[:, :-1]], axis=1)
        upper_sub = jnp.concatenate([face_slots(0)[:, 1:], blank_faces[:, :1]], axis=1)
        lower_cluster = jnp.concatenate([blank_faces[:1], face_slots(3)[:-1]], axis=0)
        upper_cluster = jnp.concatenate([face_slots(2)[1:], blank_faces[:1]], axis=0)
        return jnp.concatenate([lower_sub, upper_sub, lower_cluster, upper_cluster, blank_faces, blank_faces, face_slots(7), face_slots(6)], axis=2)

    def assemble(values):
        width_now = values.shape[-1]
        blocks = values.reshape(device_total, block_total, BLK, width_now)
        sent = jnp.take_along_axis(blocks, slot_block[:, :, None, None], axis=1)
        slot_grid = sent.reshape(N_CLUSTER, N_SUB, block_total, BLK, width_now)
        received = receive(slot_grid).reshape(sent.shape)
        assembled = jnp.take_along_axis(sent - received, inverse[:, :, None, None], axis=1)
        return assembled.reshape(N_SUBDOM, M, width_now)

    def apply_dual(direction):
        rounded = lax.optimization_barrier(direction.astype(jnp.bfloat16)).astype(jnp.float32)

        def apply_one(paired):
            return jnp.dot(paired[0].astype(jnp.float32), paired[1], precision=highest)

        return assemble(lax.map(apply_one, (dual_operators, rounded)))

    def coarse_coefficients(values):
        coarse_terms = jnp.einsum("srm,sml->srl", modes, values, precision=highest).reshape(NC, LOADS)
        return jnp.dot(coarse_matrix, coarse_terms, precision=highest)

    def spread_modes(coeff):
        return jnp.einsum("srm,srl->sml", modes, coeff.reshape(N_SUBDOM, NMODE, LOADS), precision=highest)

    def project(values):
        return values - assemble(spread_modes(coarse_coefficients(values)))

    def inner_product(left, right):
        return jnp.sum(weights[:, :, None] * left * right, axis=(0, 1))

    dual_rhs = assemble(local_loads)
    multipliers = assemble(spread_modes(jnp.dot(coarse_matrix, coarse_loads, precision=highest)))
    residual = dual_rhs - apply_dual(multipliers)
    projected = project(residual)
    gamma_now = inner_product(projected, projected)
    direction = projected
    for iteration in range(ITERS):
        image_dir = apply_dual(direction)
        step_size = gamma_now / inner_product(direction, image_dir)
        multipliers = multipliers + step_size * direction
        residual = residual - step_size * image_dir
        projected = project(residual)
        if iteration + 1 < ITERS:
            gamma_next = inner_product(projected, projected)
            direction = projected + (gamma_next / gamma_now) * direction
            gamma_now = gamma_next
    return (multipliers, projected)
```

```python
import jax
import jax.numpy as jnp
from jax import lax
from jax.experimental import pallas as pl
from jax.experimental.pallas import tpu as pltpu
from jax.sharding import PartitionSpec as P

NMODE = 6
ITERS = 3
BLK = 128
GRP = 16
NGRP = 5
ROWS = GRP * NGRP
F32, BF16 = jnp.float32, jnp.bfloat16
HIGHEST = lax.Precision.HIGHEST


def dot(a, b):
    return jnp.dot(a, b, preferred_element_type=F32)


def split(x):
    hi = x.astype(BF16)
    return hi, (x - hi.astype(F32)).astype(BF16)


def stacked(a):
    hi, lo = split(a)
    return jnp.concatenate([hi, hi, lo, jnp.zeros((256 - 3 * ROWS, a.shape[1]), BF16)], axis=0)


def params(mib):
    return pltpu.CompilerParams(dimension_semantics=("arbitrary",), vmem_limit_bytes=mib << 20)


def whole(shape):
    return pl.BlockSpec(shape, lambda *_: (0,) * len(shape))


def shape(dims, dtype=F32):
    return jax.ShapeDtypeStruct(dims, dtype)


def prep_body(slot, modes, coarse, rs, p0, p1, p2, p3):
    payloads = (p0, p1, p2, p3)
    nc = coarse.shape[1]
    for p in payloads:
        p[0:12, 0:nc] = coarse[...]
        p[12:16, 0:nc] = jnp.zeros((4, nc), F32)
    for s in range(32):
        b = slot[s]
        t, j = b // 16, b % 16
        at = pl.ds(pl.multiple_of(j * BLK, BLK), BLK)
        rs[s] = jnp.zeros((GRP, BLK), F32)
        rs[s, 0:6, :] = jnp.where(t == 0, modes[0, :, at], 0.0)
        rs[s, 6:12, :] = jnp.where(t == 1, modes[1, :, at], 0.0)
        if s < 16:
            payloads[s // 4][:, nc + (s % 4) * BLK : nc + (s % 4 + 1) * BLK] = rs[s]


def prep(slot, modes, coarse):
    nc = coarse.shape[1]
    return pl.pallas_call(
        prep_body,
        grid_spec=pltpu.PrefetchScalarGridSpec(
            num_scalar_prefetch=1,
            grid=(1,),
            in_specs=[whole(modes.shape), whole(coarse.shape)],
            out_specs=[whole((32, GRP, BLK))] + [whole((GRP, nc + 4 * BLK))] * 4,
        ),
        out_shape=[shape((32, GRP, BLK))] + [shape((GRP, nc + 4 * BLK))] * 4,
        compiler_params=params(16),
    )(slot, modes, coarse)


def init_body(slot, wm, rs, q0, q1, q2, q3, coarse, loads, bcat, bt2, c2, lam, xb, c60, bt):
    received = (q0, q1, q2, q3)
    nc = coarse.shape[1]
    c60[...] = jnp.zeros(c60.shape, F32)
    c60[0:12, :] = coarse[...]
    for g in range(4):
        c60[GRP * (g + 1) : GRP * (g + 2), :] = received[g][:, 0:nc]
    hi, lo = split(c60[...])
    c2[0:ROWS, :] = hi
    c2[ROWS:, :] = lo
    a = jnp.dot(c60[...], loads[...], precision=HIGHEST, preferred_element_type=F32)
    acat = stacked(a)
    for s in range(32):
        f, k = s // 4, s % 4
        bt[...] = jnp.zeros(bt.shape, F32)
        own = rs[s]
        if f >= 6:
            own = own - rs[s + 4 if f == 6 else s - 4]
        bt[0:GRP, :] = own
        if f < 4:
            bt[GRP * (f + 1) : GRP * (f + 2), :] = -wm[8 + f] * received[f][:, nc + k * BLK : nc + (k + 1) * BLK]
        v = bt[...]
        vh = v.astype(BF16)
        vhf = vh.astype(F32)
        vl = v - vhf
        bt2[s, 0:ROWS, :] = vh
        bt2[s, ROWS:, :] = vl.astype(BF16)
        tall = jnp.concatenate([vhf, vl, vhf, jnp.zeros((256 - 3 * ROWS, BLK), F32)], axis=0)
        wide = tall.T.astype(BF16)
        bcat[s] = wide
        x = dot(wide, acat)
        lam[s] = x
        xb[slot[s]] = x.astype(BF16)


def initial(slot, wm, rs, received, coarse, coarse_loads):
    nc = coarse.shape[1]
    args = (rs, *received, coarse, coarse_loads)
    outs = [
        shape((32, BLK, 256), BF16),
        shape((32, 2 * ROWS, BLK), BF16),
        shape((2 * ROWS, nc), BF16),
        shape((32, BLK, BLK)),
        shape((32, BLK, BLK), BF16),
    ]
    return pl.pallas_call(
        init_body,
        grid_spec=pltpu.PrefetchScalarGridSpec(
            num_scalar_prefetch=2,
            grid=(1,),
            in_specs=[whole(x.shape) for x in args],
            out_specs=[whole(x.shape) for x in outs],
            scratch_shapes=[pltpu.VMEM((ROWS, nc), F32), pltpu.VMEM((ROWS, BLK), F32)],
        ),
        out_shape=outs,
        compiler_params=params(32),
    )(slot, wm, *args)


def apply_body(first, inv, k_ref, x_ref, bt2, *refs):
    if first:
        loads, y, y0, y1, y2, y3, eo, el, er, ed, eu, acc, dacc = refs
    else:
        u0, u1, u2, u3, part, y, y0, y1, y2, y3, eo, el, er, ed, eu, acc, dacc = refs
        us = (u0, u1, u2, u3)
    i = pl.program_id(0)

    @pl.when(i == 0)
    def _():
        acc[...] = jnp.zeros(acc.shape, F32)
        dacc[...] = jnp.zeros(dacc.shape, F32)

    tile = dot(k_ref[0], x_ref[0])
    total = acc[...]
    delta = dacc[...]
    for j in range(4):
        s = inv[4 * i + j]
        yb = tile[j * BLK : (j + 1) * BLK]
        if first:
            yb = loads[j] - yb
        else:
            delta = delta + jnp.sum((us[j][0] * yb).reshape(16, 8, BLK), axis=0)
        y[s] = yb
        hi, lo = split(yb)
        both = dot(bt2[s], hi)
        total = total + (both[:ROWS] + both[ROWS:]) + dot(bt2[s, 0:ROWS, :], lo)
    acc[...] = total
    dacc[...] = delta

    @pl.when(i == pl.num_programs(0) - 1)
    def _():
        for f, out in enumerate((y0, y1, y2, y3)):
            out[...] = y[4 * f : 4 * f + 4]
        own = acc[0:GRP, :]
        if not first:
            rows = lax.broadcasted_iota(jnp.int32, (GRP, BLK), 0)
            own = jnp.where(rows == 12, jnp.sum(dacc[...], axis=0, keepdims=True), own)
            own = jnp.where(rows == 13, part[0:1, :], own)
            own = jnp.where(rows == 14, part[1:2, :], own)
        eo[...] = own
        for g, out in enumerate((el, er, ed, eu)):
            out[...] = acc[GRP * (g + 1) : GRP * (g + 2), :]


def apply_dual(inv, k, xb, bt2, loads=None, u=None, part=None):
    first = loads is not None
    order = k.shape[1]
    tiles = order // 512
    args = [k, xb.reshape(k.shape[0], order, BLK), bt2]
    specs = [
        pl.BlockSpec((1, 512, order), lambda i, inv: (i // tiles, i % tiles, 0)),
        pl.BlockSpec((1, order, BLK), lambda i, inv: (i // tiles, 0, 0)),
        whole(bt2.shape),
    ]
    if first:
        args.append(loads.reshape(32, BLK, BLK))
        specs.append(pl.BlockSpec((4, BLK, BLK), lambda i, inv: (i, 0, 0)))
    else:
        for j in range(4):
            args.append(u)
            specs.append(pl.BlockSpec((1, BLK, BLK), lambda i, inv, j=j: (inv[4 * i + j], 0, 0)))
        args.append(part)
        specs.append(whole(part.shape))
    outs = [shape((32, BLK, BLK))] + [shape((4, BLK, BLK))] * 4 + [shape((GRP, BLK))] * 5
    return pl.pallas_call(
        lambda *refs: apply_body(first, *refs),
        grid_spec=pltpu.PrefetchScalarGridSpec(
            num_scalar_prefetch=1,
            grid=(8,),
            in_specs=specs,
            out_specs=[whole(x.shape) for x in outs],
            scratch_shapes=[pltpu.VMEM((ROWS, BLK), F32), pltpu.VMEM((8, BLK), F32)],
        ),
        out_shape=outs,
        compiler_params=params(24),
        name="apply_first" if first else "apply",
    )(inv, *args)


def update_body(kind, slot, tab, wm, *refs):
    first, last, chained = kind == 0, kind == ITERS, kind >= 2
    refs = list(refs)
    take = lambda n: [refs.pop(0) for _ in range(n)]
    h, c2, r0, r1, r2, r3, y, yp, bcat = take(9)
    if not first:
        (u,) = take(1)
    if chained:
        img_in, a_in, scal_in = take(3)
    if last:
        lam_in, d_in = take(2)
        lam_out, u_out = take(2)
    elif first:
        u_out, xb, part = take(3)
    else:
        u_out, xb, part, img_out, a_out, scal = take(6)
    habs, acat, pr, coef, sums = take(5)
    f = pl.program_id(0)

    @pl.when(f == 0)
    def _():
        tail = jnp.zeros((8, BLK), F32)
        for j in range(128):
            piece = h[tab[j]]
            habs[12 * j : 12 * j + 12, :] = piece[0:12]
            tail = tail + piece[8:16]
        hi, lo = split(habs[...])
        both = dot(c2[...], hi)
        a = both[:ROWS] + both[ROWS:] + dot(c2[0:ROWS, :], lo)
        sums[...] = jnp.zeros(sums.shape, F32)
        if not first:
            delta, gamma, eps = tail[4:5], tail[5:6], tail[6:7]
            if chained:
                beta = gamma / scal_in[0:1, :]
                curve = delta + 2.0 * beta * eps + beta * beta * scal_in[1:2, :]
                a = a + beta * a_in[...]
                coef[1:2, :] = beta
            else:
                curve = delta
            step = gamma / curve
            coef[0:1, :] = step
            if not last:
                a_out[...] = a
                scal[...] = jnp.zeros(scal.shape, F32)
                scal[0:1, :] = gamma
                scal[1:2, :] = curve
                scal[2:3, :] = step
                if chained:
                    scal[3:4, :] = beta
        acat[...] = stacked(a)

    for g, r in enumerate((r0, r1, r2, r3)):

        @pl.when(f == g)
        def _():
            pr[...] = r[...] * wm[8 + g]

    @pl.when((f == 4) | (f == 5))
    def _():
        pr[...] = jnp.zeros(pr.shape, F32)

    @pl.when(f >= 6)
    def _():
        pr[...] = yp[...]

    w = wm[f]
    for k in range(4):
        image = y[k] - pr[k]
        if chained:
            image = image + coef[1:2, :] * img_in[k]
        fix = dot(bcat[k], acat[...])
        if first:
            new = image - fix
        else:
            new = u[k] - coef[0:1, :] * (image - fix)
        b = slot[4 * f + k]
        if last:
            direction = u[k] + coef[1:2, :] * d_in[k]
            lam_out[b] = lam_in[k] + coef[0:1, :] * direction
            u_out[b] = new
        else:
            u_out[k] = new
            xb[b] = new.astype(BF16)
            weighted = new * w
            sums[0:8, :] += jnp.sum((weighted * new).reshape(16, 8, BLK), axis=0)
            if not first:
                img_out[k] = image
                sums[8:16, :] += jnp.sum((weighted * image).reshape(16, 8, BLK), axis=0)

    if not last:

        @pl.when(f == pl.num_programs(0) - 1)
        def _():
            part[...] = jnp.zeros(part.shape, F32)
            part[0:1, :] = jnp.sum(sums[0:8, :], axis=0, keepdims=True)
            part[1:2, :] = jnp.sum(sums[8:16, :], axis=0, keepdims=True)


def update(kind, slot, tab, wm, h, c2, received, y, bcat, u=None, chain=None, closing=None):
    first, last, chained = kind == 0, kind == ITERS, kind >= 2
    face = pl.BlockSpec((4, BLK, BLK), lambda f, *_: (f, 0, 0))
    args = [h, c2, *received, y, y, bcat]
    specs = [whole(x.shape) for x in args[:6]]
    specs += [
        face,
        pl.BlockSpec((4, BLK, BLK), lambda f, *_: (jnp.where(f >= 6, 13 - f, 7), 0, 0)),
        pl.BlockSpec((4, BLK, 256), lambda f, *_: (f, 0, 0)),
    ]
    if not first:
        args.append(u)
        specs.append(face)
    if chained:
        args += list(chain)
        specs += [face, whole(chain[1].shape), whole(chain[2].shape)]
    vector, small = shape((32, BLK, BLK)), shape((8, BLK))
    if last:
        args += list(closing)
        specs += [face, face]
        outs, out_specs = [vector, vector], [whole(vector.shape)] * 2
    else:
        outs = [vector, shape((32, BLK, BLK), BF16), small]
        out_specs = [face, whole(vector.shape), whole(small.shape)]
        if not first:
            outs += [vector, shape((ROWS, BLK)), small]
            out_specs += [face, whole((ROWS, BLK)), whole(small.shape)]
    return pl.pallas_call(
        lambda *refs: update_body(kind, *refs),
        grid_spec=pltpu.PrefetchScalarGridSpec(
            num_scalar_prefetch=3,
            grid=(8,),
            in_specs=specs,
            out_specs=out_specs,
            scratch_shapes=[
                pltpu.VMEM((c2.shape[1], BLK), F32),
                pltpu.VMEM((256, BLK), BF16),
                pltpu.VMEM((4, BLK, BLK), F32),
                pltpu.VMEM((8, BLK), F32),
                pltpu.VMEM((16, BLK), F32),
            ],
        ),
        out_shape=outs,
        compiler_params=params(24),
        name=f"update_{kind}",
    )(slot, tab, wm, *args)


def on_device(dual_operators, local_loads, modes, coarse_matrix, coarse_loads, slot_block):
    n_sub, n_cluster = lax.axis_size("sub"), lax.axis_size("cluster")
    own, cluster = lax.axis_index("sub"), lax.axis_index("cluster")
    slot = slot_block[0]
    positions = jnp.arange(32, dtype=jnp.int32)
    inv = jnp.sum(positions[:, None] * (slot[:, None] == positions[None, :]).astype(jnp.int32), axis=0)
    there = jnp.stack([own > 0, own < n_sub - 1, cluster > 0, cluster < n_cluster - 1])
    one = jnp.ones((4,), F32)
    wm = jnp.concatenate([jnp.where(there, 0.5, 1.0), jnp.array([1.0, 1.0, 0.5, 0.5]), there.astype(F32), one]).astype(F32)

    device = jnp.arange(n_sub * n_cluster, dtype=jnp.int32)
    dz, dsub = device // n_sub, device % n_sub
    far = lambda now, mine: (now - mine) % 4
    tab = (
        (((dsub % 2) ^ (own % 2)) * 4 + far(dsub // 2 % 4, own // 2 % 4)) * 4 + far(dsub // 8, own // 8)
    ) * 4 + far(dz, cluster)

    def along_sub(value, source):
        return lax.ppermute(value, "sub", [(source(i), i) for i in range(n_sub)])

    def along_cluster(value, k):
        return lax.ppermute(value, "cluster", [((i + k) % n_cluster, i) for i in range(n_cluster)])

    def exchange(p0, p1, p2, p3):
        return [
            along_sub(p1, lambda i: (i - 1) % n_sub),
            along_sub(p0, lambda i: (i + 1) % n_sub),
            along_cluster(p3, -1),
            along_cluster(p2, 1),
        ]

    def gather(faces, groups):
        eo, el, er, ed, eu = groups
        mine = eo + along_sub(er, lambda i: (i - 1) % n_sub) + along_sub(el, lambda i: (i + 1) % n_sub)
        sent = lax.optimization_barrier(jnp.concatenate([mine, ed, eu], axis=0))
        z = [sent] + [along_cluster(sent, k) for k in (1, 2, 3)]
        z, faces = lax.optimization_barrier((z, faces))
        received = exchange(*faces)
        h = [z[k][:GRP] + z[(k + 1) % 4][GRP : 2 * GRP] + z[(k + 3) % 4][2 * GRP :] for k in range(4)]
        h = lax.optimization_barrier(jnp.concatenate(h, axis=0))
        for step in (8, 2):
            place = lambda i, k: i - i % (4 * step) + (i + k * step) % (4 * step)
            h = [h] + [along_sub(h, lambda i, k=k: place(i, k)) for k in (1, 2, 3)]
            h = lax.optimization_barrier(jnp.concatenate(h, axis=0))
        h = jnp.concatenate([h, along_sub(h, lambda i: i ^ 1)], axis=0)
        return h.reshape(128, GRP, BLK), received

    rs, *payload = prep(slot, modes, coarse_matrix)
    neighbours = exchange(*payload)
    bcat, bt2, c2, lam, xb = initial(slot, wm, rs, neighbours, coarse_matrix, coarse_loads)

    y, *sent = apply_dual(inv, dual_operators, xb, bt2, loads=local_loads)
    h, received = gather(sent[:4], sent[4:])
    u, xb, part = update(0, slot, tab, wm, h, c2, received, y, bcat)
    chain, direction = None, None
    for kind in range(1, ITERS + 1):
        y, *sent = apply_dual(inv, dual_operators, xb, bt2, u=u, part=part)
        h, received = gather(sent[:4], sent[4:])
        closing = (lam, direction) if kind == ITERS else None
        outs = update(kind, slot, tab, wm, h, c2, received, y, bcat, u, chain, closing)
        if kind < ITERS:
            new, xb, part, image, a, scal = outs
            direction = u if direction is None else u + scal[3] * direction
            lam = lam + scal[2] * direction
            u, chain = new, (image, a, scal)
    shape_out = local_loads.shape
    return outs[0].reshape(shape_out), outs[1].reshape(shape_out)


def solution(mesh):
    spec = P(("cluster", "sub"), None, None)
    flat = P(("cluster", "sub"), None)
    return jax.shard_map(
        on_device,
        mesh=mesh,
        in_specs=(spec, spec, spec, flat, P(), flat),
        out_specs=(spec, spec),
        check_vma=False,
    )
```

```python
import jax
import jax.numpy as jnp
from jax import lax
from jax.experimental import pallas as pl
from jax.experimental.pallas import tpu as pltpu
from jax.sharding import PartitionSpec as P

NMODE = 6
ITERS = 3
BLK = 128
GRP = 16
NGRP = 5
ROWS = GRP * NGRP
F32, BF16 = jnp.float32, jnp.bfloat16
HIGHEST = lax.Precision.HIGHEST


def dot(a, b):
    return jnp.dot(a, b, preferred_element_type=F32)


def split(x):
    hi = x.astype(BF16)
    return hi, (x - hi.astype(F32)).astype(BF16)


def stacked(a):
    hi, lo = split(a)
    return jnp.concatenate([hi, hi, lo, jnp.zeros((256 - 3 * ROWS, a.shape[1]), BF16)], axis=0)


def hbm(x):
    return pltpu.with_memory_space_constraint(x, pltpu.HBM)


def params(mib):
    return pltpu.CompilerParams(dimension_semantics=("arbitrary",), vmem_limit_bytes=mib << 20)


def whole(shape, **mode):
    return pl.BlockSpec(shape, lambda *_: (0,) * len(shape), **mode)


def held(shape):
    return whole(shape, pipeline_mode=pl.Buffered(1))


def shape(dims, dtype=F32):
    return jax.ShapeDtypeStruct(dims, dtype)


def prep_body(slot, modes, coarse, rs, p0, p1, p2, p3):
    payloads = (p0, p1, p2, p3)
    nc = coarse.shape[1]
    for p in payloads:
        p[0:12, 0:nc] = coarse[...]
        p[12:16, 0:nc] = jnp.zeros((4, nc), F32)
    for s in range(32):
        b = slot[s]
        t, j = b // 16, b % 16
        at = pl.ds(pl.multiple_of(j * BLK, BLK), BLK)
        rs[s] = jnp.zeros((GRP, BLK), F32)
        rs[s, 0:6, :] = jnp.where(t == 0, modes[0, :, at], 0.0)
        rs[s, 6:12, :] = jnp.where(t == 1, modes[1, :, at], 0.0)
        if s < 16:
            payloads[s // 4][:, nc + (s % 4) * BLK : nc + (s % 4 + 1) * BLK] = rs[s]


def prep(slot, modes, coarse):
    nc = coarse.shape[1]
    return pl.pallas_call(
        prep_body,
        grid_spec=pltpu.PrefetchScalarGridSpec(
            num_scalar_prefetch=1,
            grid=(1,),
            in_specs=[held(modes.shape), held(coarse.shape)],
            out_specs=[whole((32, GRP, BLK))] + [whole((GRP, nc + 4 * BLK))] * 4,
        ),
        out_shape=[shape((32, GRP, BLK))] + [shape((GRP, nc + 4 * BLK))] * 4,
        compiler_params=params(6),
    )(slot, hbm(modes), hbm(coarse))


def init_body(slot, wm, rs, q0, q1, q2, q3, coarse, loads, bcat, bt2, c2, lam, xb, c60, bt):
    received = (q0, q1, q2, q3)
    nc = coarse.shape[1]
    c60[...] = jnp.zeros(c60.shape, F32)
    c60[0:12, :] = coarse[...]
    for g in range(4):
        c60[GRP * (g + 1) : GRP * (g + 2), :] = received[g][:, 0:nc]
    hi, lo = split(c60[...])
    c2[0:ROWS, :] = hi
    c2[ROWS:, :] = lo
    a = jnp.dot(c60[...], loads[...], precision=HIGHEST, preferred_element_type=F32)
    acat = stacked(a)
    for s in range(32):
        f, k = s // 4, s % 4
        bt[...] = jnp.zeros(bt.shape, F32)
        own = rs[s]
        if f >= 6:
            own = own - rs[s + 4 if f == 6 else s - 4]
        bt[0:GRP, :] = own
        if f < 4:
            bt[GRP * (f + 1) : GRP * (f + 2), :] = -wm[8 + f] * received[f][:, nc + k * BLK : nc + (k + 1) * BLK]
        v = bt[...]
        vh = v.astype(BF16)
        vhf = vh.astype(F32)
        vl = v - vhf
        bt2[s, 0:ROWS, :] = vh
        bt2[s, ROWS:, :] = vl.astype(BF16)
        tall = jnp.concatenate([vhf, vl, vhf, jnp.zeros((256 - 3 * ROWS, BLK), F32)], axis=0)
        wide = tall.T.astype(BF16)
        bcat[s] = wide
        x = dot(wide, acat)
        lam[s] = x
        xb[slot[s]] = x.astype(BF16)


def initial(slot, wm, rs, received, coarse, coarse_loads):
    nc = coarse.shape[1]
    args = tuple(hbm(x) for x in (rs, *received, coarse, coarse_loads))
    outs = [
        shape((32, BLK, 256), BF16),
        shape((32, 2 * ROWS, BLK), BF16),
        shape((2 * ROWS, nc), BF16),
        shape((32, BLK, BLK)),
        shape((32, BLK, BLK), BF16),
    ]
    return pl.pallas_call(
        init_body,
        grid_spec=pltpu.PrefetchScalarGridSpec(
            num_scalar_prefetch=2,
            grid=(1,),
            in_specs=[held(x.shape) for x in args],
            out_specs=[whole(x.shape) for x in outs],
            scratch_shapes=[pltpu.VMEM((ROWS, nc), F32), pltpu.VMEM((ROWS, BLK), F32)],
        ),
        out_shape=outs,
        compiler_params=params(16),
    )(slot, wm, *args)


def apply_body(first, inv, k_ref, x_ref, bt2, *refs):
    if first:
        loads, y, y0, y1, y2, y3, eo, el, er, ed, eu, acc, dacc = refs
    else:
        u0, u1, u2, u3, part, y, y0, y1, y2, y3, eo, el, er, ed, eu, acc, dacc = refs
        us = (u0, u1, u2, u3)
    i = pl.program_id(0)

    @pl.when(i == 0)
    def _():
        acc[...] = jnp.zeros(acc.shape, F32)
        dacc[...] = jnp.zeros(dacc.shape, F32)

    tile = dot(k_ref[0], x_ref[0])
    total = acc[...]
    delta = dacc[...]
    for j in range(4):
        s = inv[4 * i + j]
        yb = tile[j * BLK : (j + 1) * BLK]
        if first:
            yb = loads[j] - yb
        else:
            delta = delta + jnp.sum((us[j][0] * yb).reshape(16, 8, BLK), axis=0)
        y[s] = yb
        hi, lo = split(yb)
        both = dot(bt2[s], hi)
        total = total + (both[:ROWS] + both[ROWS:]) + dot(bt2[s, 0:ROWS, :], lo)
    acc[...] = total
    dacc[...] = delta

    @pl.when(i == pl.num_programs(0) - 1)
    def _():
        for f, out in enumerate((y0, y1, y2, y3)):
            out[...] = y[4 * f : 4 * f + 4]
        own = acc[0:GRP, :]
        if not first:
            rows = lax.broadcasted_iota(jnp.int32, (GRP, BLK), 0)
            own = jnp.where(rows == 12, jnp.sum(dacc[...], axis=0, keepdims=True), own)
            own = jnp.where(rows == 13, part[0:1, :], own)
            own = jnp.where(rows == 14, part[1:2, :], own)
        eo[...] = own
        for g, out in enumerate((el, er, ed, eu)):
            out[...] = acc[GRP * (g + 1) : GRP * (g + 2), :]


def apply_dual(inv, k, xb, bt2, loads=None, u=None, part=None):
    first = loads is not None
    order = k.shape[1]
    tiles = order // 512
    args = [k, xb.reshape(k.shape[0], order, BLK), bt2]
    specs = [
        pl.BlockSpec((1, 512, order), lambda i, inv: (i // tiles, i % tiles, 0)),
        pl.BlockSpec((1, order, BLK), lambda i, inv: (i // tiles, 0, 0)),
        held(bt2.shape),
    ]
    if first:
        args.append(loads.reshape(32, BLK, BLK))
        specs.append(pl.BlockSpec((4, BLK, BLK), lambda i, inv: (i, 0, 0)))
    else:
        for j in range(4):
            args.append(u)
            specs.append(pl.BlockSpec((1, BLK, BLK), lambda i, inv, j=j: (inv[4 * i + j], 0, 0)))
        args.append(part)
        specs.append(held(part.shape))
    outs = [shape((32, BLK, BLK))] + [shape((4, BLK, BLK))] * 4 + [shape((GRP, BLK))] * 5
    return pl.pallas_call(
        lambda *refs: apply_body(first, *refs),
        grid_spec=pltpu.PrefetchScalarGridSpec(
            num_scalar_prefetch=1,
            grid=(8,),
            in_specs=specs,
            out_specs=[whole(x.shape) for x in outs],
            scratch_shapes=[pltpu.VMEM((ROWS, BLK), F32), pltpu.VMEM((8, BLK), F32)],
        ),
        out_shape=outs,
        compiler_params=params(16),
        name="apply_first" if first else "apply",
    )(inv, *args)


def update_body(kind, slot, tab, wm, *refs):
    first, last, chained = kind == 0, kind == ITERS, kind >= 2
    refs = list(refs)
    take = lambda n: [refs.pop(0) for _ in range(n)]
    h, c2, r0, r1, r2, r3, y, yp, bcat = take(9)
    if not first:
        (u,) = take(1)
    if chained:
        img_in, a_in, scal_in = take(3)
    if last:
        lam_in, d_in = take(2)
        lam_out, u_out = take(2)
    elif first:
        u_out, xb, part = take(3)
    else:
        u_out, xb, part, img_out, a_out, scal = take(6)
    habs, acat, pr, coef, sums = take(5)
    f = pl.program_id(0)

    @pl.when(f == 0)
    def _():
        tail = jnp.zeros((8, BLK), F32)
        for j in range(128):
            piece = h[tab[j]]
            habs[12 * j : 12 * j + 12, :] = piece[0:12]
            tail = tail + piece[8:16]
        hi, lo = split(habs[...])
        both = dot(c2[...], hi)
        a = both[:ROWS] + both[ROWS:] + dot(c2[0:ROWS, :], lo)
        sums[...] = jnp.zeros(sums.shape, F32)
        if not first:
            delta, gamma, eps = tail[4:5], tail[5:6], tail[6:7]
            if chained:
                beta = gamma / scal_in[0:1, :]
                curve = delta + 2.0 * beta * eps + beta * beta * scal_in[1:2, :]
                a = a + beta * a_in[...]
                coef[1:2, :] = beta
            else:
                curve = delta
            step = gamma / curve
            coef[0:1, :] = step
            if not last:
                a_out[...] = a
                scal[...] = jnp.zeros(scal.shape, F32)
                scal[0:1, :] = gamma
                scal[1:2, :] = curve
                scal[2:3, :] = step
                if chained:
                    scal[3:4, :] = beta
        acat[...] = stacked(a)

    for g, r in enumerate((r0, r1, r2, r3)):

        @pl.when(f == g)
        def _():
            pr[...] = r[...] * wm[8 + g]

    @pl.when((f == 4) | (f == 5))
    def _():
        pr[...] = jnp.zeros(pr.shape, F32)

    @pl.when(f >= 6)
    def _():
        pr[...] = yp[...]

    w = wm[f]
    for k in range(4):
        image = y[k] - pr[k]
        if chained:
            image = image + coef[1:2, :] * img_in[k]
        fix = dot(bcat[k], acat[...])
        if first:
            new = image - fix
        else:
            new = u[k] - coef[0:1, :] * (image - fix)
        b = slot[4 * f + k]
        if last:
            direction = u[k] + coef[1:2, :] * d_in[k]
            lam_out[b] = lam_in[k] + coef[0:1, :] * direction
            u_out[b] = new
        else:
            u_out[k] = new
            xb[b] = new.astype(BF16)
            weighted = new * w
            sums[0:8, :] += jnp.sum((weighted * new).reshape(16, 8, BLK), axis=0)
            if not first:
                img_out[k] = image
                sums[8:16, :] += jnp.sum((weighted * image).reshape(16, 8, BLK), axis=0)

    if not last:

        @pl.when(f == pl.num_programs(0) - 1)
        def _():
            part[...] = jnp.zeros(part.shape, F32)
            part[0:1, :] = jnp.sum(sums[0:8, :], axis=0, keepdims=True)
            part[1:2, :] = jnp.sum(sums[8:16, :], axis=0, keepdims=True)


def update(kind, slot, tab, wm, h, c2, received, y, bcat, u=None, chain=None, closing=None):
    first, last, chained = kind == 0, kind == ITERS, kind >= 2
    face = pl.BlockSpec((4, BLK, BLK), lambda f, *_: (f, 0, 0))
    args = [h, c2, *received, y, y, bcat]
    specs = [held(x.shape) for x in args[:6]]
    specs += [
        face,
        pl.BlockSpec((4, BLK, BLK), lambda f, *_: (jnp.where(f >= 6, 13 - f, 7), 0, 0)),
        pl.BlockSpec((4, BLK, 256), lambda f, *_: (f, 0, 0)),
    ]
    if not first:
        args.append(u)
        specs.append(face)
    if chained:
        args += list(chain)
        specs += [face, held(chain[1].shape), held(chain[2].shape)]
    vector, small = shape((32, BLK, BLK)), shape((8, BLK))
    if last:
        args += list(closing)
        specs += [face, face]
        outs, out_specs = [vector, vector], [whole(vector.shape)] * 2
    else:
        outs = [vector, shape((32, BLK, BLK), BF16), small]
        out_specs = [face, whole(vector.shape), whole(small.shape)]
        if not first:
            outs += [vector, shape((ROWS, BLK)), small]
            out_specs += [face, whole((ROWS, BLK)), whole(small.shape)]
    return pl.pallas_call(
        lambda *refs: update_body(kind, *refs),
        grid_spec=pltpu.PrefetchScalarGridSpec(
            num_scalar_prefetch=3,
            grid=(8,),
            in_specs=specs,
            out_specs=out_specs,
            scratch_shapes=[
                pltpu.VMEM((c2.shape[1], BLK), F32),
                pltpu.VMEM((256, BLK), BF16),
                pltpu.VMEM((4, BLK, BLK), F32),
                pltpu.VMEM((8, BLK), F32),
                pltpu.VMEM((16, BLK), F32),
            ],
        ),
        out_shape=outs,
        compiler_params=params(16),
        name=f"update_{kind}",
    )(slot, tab, wm, *args)


def on_device(dual_operators, local_loads, modes, coarse_matrix, coarse_loads, slot_block):
    n_sub, n_cluster = lax.axis_size("sub"), lax.axis_size("cluster")
    own, cluster = lax.axis_index("sub"), lax.axis_index("cluster")
    slot = slot_block[0]
    positions = jnp.arange(32, dtype=jnp.int32)
    inv = jnp.sum(positions[:, None] * (slot[:, None] == positions[None, :]).astype(jnp.int32), axis=0)
    there = jnp.stack([own > 0, own < n_sub - 1, cluster > 0, cluster < n_cluster - 1])
    one = jnp.ones((4,), F32)
    wm = jnp.concatenate([jnp.where(there, 0.5, 1.0), jnp.array([1.0, 1.0, 0.5, 0.5]), there.astype(F32), one]).astype(F32)

    device = jnp.arange(n_sub * n_cluster, dtype=jnp.int32)
    dz, dsub = device // n_sub, device % n_sub
    far = lambda now, mine: (now - mine) % 4
    tab = (
        (((dsub % 2) ^ (own % 2)) * 4 + far(dsub // 2 % 4, own // 2 % 4)) * 4 + far(dsub // 8, own // 8)
    ) * 4 + far(dz, cluster)

    def along_sub(value, source):
        return lax.ppermute(value, "sub", [(source(i), i) for i in range(n_sub)])

    def along_cluster(value, k):
        return lax.ppermute(value, "cluster", [((i + k) % n_cluster, i) for i in range(n_cluster)])

    def exchange(p0, p1, p2, p3):
        return [
            along_sub(p1, lambda i: (i - 1) % n_sub),
            along_sub(p0, lambda i: (i + 1) % n_sub),
            along_cluster(p3, -1),
            along_cluster(p2, 1),
        ]

    def gather(faces, groups):
        eo, el, er, ed, eu = groups
        mine = eo + along_sub(er, lambda i: (i - 1) % n_sub) + along_sub(el, lambda i: (i + 1) % n_sub)
        sent = lax.optimization_barrier(jnp.concatenate([mine, ed, eu], axis=0))
        z = [sent] + [along_cluster(sent, k) for k in (1, 2, 3)]
        mine, faces = lax.optimization_barrier((mine, faces))
        received = exchange(*faces)
        h = [z[k][:GRP] + z[(k + 1) % 4][GRP : 2 * GRP] + z[(k + 3) % 4][2 * GRP :] for k in range(4)]
        h = lax.optimization_barrier(jnp.concatenate(h, axis=0))
        for step in (8, 2):
            place = lambda i, k: i - i % (4 * step) + (i + k * step) % (4 * step)
            h = [h] + [along_sub(h, lambda i, k=k: place(i, k)) for k in (1, 2, 3)]
            h = jnp.concatenate(h, axis=0)
            h, received = lax.optimization_barrier((h, received))
        h = jnp.concatenate([h, along_sub(h, lambda i: i ^ 1)], axis=0)
        return h.reshape(128, GRP, BLK), received

    rs, *payload = prep(slot, modes, coarse_matrix)
    neighbours = exchange(*payload)
    bcat, bt2, c2, lam, xb = initial(slot, wm, rs, neighbours, coarse_matrix, coarse_loads)

    y, *sent = apply_dual(inv, dual_operators, xb, bt2, loads=local_loads)
    h, received = gather(sent[:4], sent[4:])
    u, xb, part = update(0, slot, tab, wm, h, c2, received, y, bcat)
    chain, direction = None, None
    for kind in range(1, ITERS + 1):
        y, *sent = apply_dual(inv, dual_operators, xb, bt2, u=u, part=part)
        h, received = gather(sent[:4], sent[4:])
        closing = (lam, direction) if kind == ITERS else None
        outs = update(kind, slot, tab, wm, h, c2, received, y, bcat, u, chain, closing)
        if kind < ITERS:
            new, xb, part, image, a, scal = outs
            direction = u if direction is None else u + scal[3] * direction
            lam = lam + scal[2] * direction
            u, chain = new, (image, a, scal)
    shape_out = local_loads.shape
    return outs[0].reshape(shape_out), outs[1].reshape(shape_out)


def solution(mesh):
    spec = P(("cluster", "sub"), None, None)
    flat = P(("cluster", "sub"), None)
    return jax.shard_map(
        on_device,
        mesh=mesh,
        in_specs=(spec, spec, spec, flat, P(), flat),
        out_specs=(spec, spec),
        check_vma=False,
    )
```

```python
import jax
import jax.numpy as jnp
from jax import lax
from jax.experimental import pallas as pl
from jax.experimental.pallas import tpu as pltpu
from jax.sharding import PartitionSpec as P

NMODE = 6
ITERS = 3
BLK = 128
GRP = 16
NGRP = 5
ROWS = GRP * NGRP
F32, BF16 = jnp.float32, jnp.bfloat16
HIGHEST = lax.Precision.HIGHEST


def dot(a, b):
    return jnp.dot(a, b, preferred_element_type=F32)


def split(x):
    hi = x.astype(BF16)
    return hi, (x - hi.astype(F32)).astype(BF16)


def stacked(a):
    hi, lo = split(a)
    return jnp.concatenate([hi, hi, lo, jnp.zeros((256 - 3 * ROWS, a.shape[1]), BF16)], axis=0)


def hbm(x):
    return pltpu.with_memory_space_constraint(x, pltpu.HBM)


def params(mib):
    return pltpu.CompilerParams(dimension_semantics=("arbitrary",), vmem_limit_bytes=mib << 20)


def whole(shape, **mode):
    return pl.BlockSpec(shape, lambda *_: (0,) * len(shape), **mode)


def held(shape):
    return whole(shape, pipeline_mode=pl.Buffered(1))


def shape(dims, dtype=F32):
    return jax.ShapeDtypeStruct(dims, dtype)


def prep_body(slot, modes, coarse, rs, p0, p1, p2, p3):
    payloads = (p0, p1, p2, p3)
    nc = coarse.shape[1]
    for p in payloads:
        p[0:12, 0:nc] = coarse[...]
        p[12:16, 0:nc] = jnp.zeros((4, nc), F32)
    for s in range(32):
        b = slot[s]
        t, j = b // 16, b % 16
        at = pl.ds(pl.multiple_of(j * BLK, BLK), BLK)
        rs[s] = jnp.zeros((GRP, BLK), F32)
        rs[s, 0:6, :] = jnp.where(t == 0, modes[0, :, at], 0.0)
        rs[s, 6:12, :] = jnp.where(t == 1, modes[1, :, at], 0.0)
        if s < 16:
            payloads[s // 4][:, nc + (s % 4) * BLK : nc + (s % 4 + 1) * BLK] = rs[s]


def prep(slot, modes, coarse):
    nc = coarse.shape[1]
    return pl.pallas_call(
        prep_body,
        grid_spec=pltpu.PrefetchScalarGridSpec(
            num_scalar_prefetch=1,
            grid=(1,),
            in_specs=[held(modes.shape), held(coarse.shape)],
            out_specs=[whole((32, GRP, BLK))] + [whole((GRP, nc + 4 * BLK))] * 4,
        ),
        out_shape=[shape((32, GRP, BLK))] + [shape((GRP, nc + 4 * BLK))] * 4,
        compiler_params=params(6),
    )(slot, hbm(modes), hbm(coarse))


def init_body(slot, wm, rs, q0, q1, q2, q3, coarse, loads, bcat, bt2, c2, lam, xb, c60, bt):
    received = (q0, q1, q2, q3)
    nc = coarse.shape[1]
    c60[...] = jnp.zeros(c60.shape, F32)
    c60[0:12, :] = coarse[...]
    for g in range(4):
        c60[GRP * (g + 1) : GRP * (g + 2), :] = received[g][:, 0:nc]
    hi, lo = split(c60[...])
    c2[0:ROWS, :] = hi
    c2[ROWS:, :] = lo
    a = jnp.dot(c60[...], loads[...], precision=HIGHEST, preferred_element_type=F32)
    acat = stacked(a)
    for s in range(32):
        f, k = s // 4, s % 4
        bt[...] = jnp.zeros(bt.shape, F32)
        own = rs[s]
        if f >= 6:
            own = own - rs[s + 4 if f == 6 else s - 4]
        bt[0:GRP, :] = own
        if f < 4:
            bt[GRP * (f + 1) : GRP * (f + 2), :] = -wm[8 + f] * received[f][:, nc + k * BLK : nc + (k + 1) * BLK]
        v = bt[...]
        vh = v.astype(BF16)
        vhf = vh.astype(F32)
        vl = v - vhf
        bt2[s, 0:ROWS, :] = vh
        bt2[s, ROWS:, :] = vl.astype(BF16)
        tall = jnp.concatenate([vhf, vl, vhf, jnp.zeros((256 - 3 * ROWS, BLK), F32)], axis=0)
        wide = tall.T.astype(BF16)
        bcat[s] = wide
        x = dot(wide, acat)
        lam[s] = x
        xb[slot[s]] = x.astype(BF16)


def initial(slot, wm, rs, received, coarse, coarse_loads):
    nc = coarse.shape[1]
    args = tuple(hbm(x) for x in (rs, *received, coarse, coarse_loads))
    outs = [
        shape((32, BLK, 256), BF16),
        shape((32, 2 * ROWS, BLK), BF16),
        shape((2 * ROWS, nc), BF16),
        shape((32, BLK, BLK)),
        shape((32, BLK, BLK), BF16),
    ]
    return pl.pallas_call(
        init_body,
        grid_spec=pltpu.PrefetchScalarGridSpec(
            num_scalar_prefetch=2,
            grid=(1,),
            in_specs=[held(x.shape) for x in args],
            out_specs=[whole(x.shape) for x in outs],
            scratch_shapes=[pltpu.VMEM((ROWS, nc), F32), pltpu.VMEM((ROWS, BLK), F32)],
        ),
        out_shape=outs,
        compiler_params=params(16),
    )(slot, wm, *args)


def apply_body(first, inv, k_ref, x_ref, bt2, *refs):
    if first:
        loads, y, y0, y1, y2, y3, eo, el, er, ed, eu, acc, dacc = refs
    else:
        u0, u1, u2, u3, part, y, y0, y1, y2, y3, eo, el, er, ed, eu, acc, dacc = refs
        us = (u0, u1, u2, u3)
    i = pl.program_id(0)

    @pl.when(i == 0)
    def _():
        acc[...] = jnp.zeros(acc.shape, F32)
        dacc[...] = jnp.zeros(dacc.shape, F32)

    tile = dot(k_ref[0], x_ref[0])
    total = acc[...]
    delta = dacc[...]
    for j in range(4):
        s = inv[4 * i + j]
        yb = tile[j * BLK : (j + 1) * BLK]
        if first:
            yb = loads[j] - yb
        else:
            delta = delta + jnp.sum((us[j][0] * yb).reshape(16, 8, BLK), axis=0)
        y[s] = yb
        hi, lo = split(yb)
        both = dot(bt2[s], hi)
        total = total + (both[:ROWS] + both[ROWS:]) + dot(bt2[s, 0:ROWS, :], lo)
    acc[...] = total
    dacc[...] = delta

    @pl.when(i == pl.num_programs(0) - 1)
    def _():
        for f, out in enumerate((y0, y1, y2, y3)):
            out[...] = y[4 * f : 4 * f + 4]
        own = acc[0:GRP, :]
        if not first:
            rows = lax.broadcasted_iota(jnp.int32, (GRP, BLK), 0)
            own = jnp.where(rows == 12, jnp.sum(dacc[...], axis=0, keepdims=True), own)
            own = jnp.where(rows == 13, part[0:1, :], own)
            own = jnp.where(rows == 14, part[1:2, :], own)
        eo[...] = own
        for g, out in enumerate((el, er, ed, eu)):
            out[...] = acc[GRP * (g + 1) : GRP * (g + 2), :]


def apply_dual(inv, k, xb, bt2, loads=None, u=None, part=None, stream=False):
    first = loads is not None
    if stream:
        k = hbm(k)
    order = k.shape[1]
    tiles = order // 512
    args = [k, xb.reshape(k.shape[0], order, BLK), bt2]
    specs = [
        pl.BlockSpec((1, 512, order), lambda i, inv: (i // tiles, i % tiles, 0)),
        pl.BlockSpec((1, order, BLK), lambda i, inv: (i // tiles, 0, 0)),
        held(bt2.shape),
    ]
    if first:
        args.append(loads.reshape(32, BLK, BLK))
        specs.append(pl.BlockSpec((4, BLK, BLK), lambda i, inv: (i, 0, 0)))
    else:
        for j in range(4):
            args.append(u)
            specs.append(pl.BlockSpec((1, BLK, BLK), lambda i, inv, j=j: (inv[4 * i + j], 0, 0)))
        args.append(part)
        specs.append(held(part.shape))
    outs = [shape((32, BLK, BLK))] + [shape((4, BLK, BLK))] * 4 + [shape((GRP, BLK))] * 5
    return pl.pallas_call(
        lambda *refs: apply_body(first, *refs),
        grid_spec=pltpu.PrefetchScalarGridSpec(
            num_scalar_prefetch=1,
            grid=(8,),
            in_specs=specs,
            out_specs=[whole(x.shape) for x in outs],
            scratch_shapes=[pltpu.VMEM((ROWS, BLK), F32), pltpu.VMEM((8, BLK), F32)],
        ),
        out_shape=outs,
        compiler_params=params(16),
        name="apply_first" if first else "apply",
    )(inv, *args)


def update_body(kind, slot, tab, wm, *refs):
    first, last, chained = kind == 0, kind == ITERS, kind >= 2
    refs = list(refs)
    take = lambda n: [refs.pop(0) for _ in range(n)]
    h, c2, r0, r1, r2, r3, y, yp, bcat = take(9)
    if not first:
        (u,) = take(1)
    if chained:
        img_in, a_in, scal_in = take(3)
    if last:
        lam_in, d_in = take(2)
        lam_out, u_out = take(2)
    elif first:
        u_out, xb, part = take(3)
    else:
        u_out, xb, part, img_out, a_out, scal = take(6)
    habs, acat, pr, coef, sums = take(5)
    f = pl.program_id(0)

    @pl.when(f == 0)
    def _():
        tail = jnp.zeros((8, BLK), F32)
        for j in range(128):
            piece = h[tab[j]]
            habs[12 * j : 12 * j + 12, :] = piece[0:12]
            tail = tail + piece[8:16]
        hi, lo = split(habs[...])
        both = dot(c2[...], hi)
        a = both[:ROWS] + both[ROWS:] + dot(c2[0:ROWS, :], lo)
        sums[...] = jnp.zeros(sums.shape, F32)
        if not first:
            delta, gamma, eps = tail[4:5], tail[5:6], tail[6:7]
            if chained:
                beta = gamma / scal_in[0:1, :]
                curve = delta + 2.0 * beta * eps + beta * beta * scal_in[1:2, :]
                a = a + beta * a_in[...]
                coef[1:2, :] = beta
            else:
                curve = delta
            step = gamma / curve
            coef[0:1, :] = step
            if not last:
                a_out[...] = a
                scal[...] = jnp.zeros(scal.shape, F32)
                scal[0:1, :] = gamma
                scal[1:2, :] = curve
                scal[2:3, :] = step
                if chained:
                    scal[3:4, :] = beta
        acat[...] = stacked(a)

    for g, r in enumerate((r0, r1, r2, r3)):

        @pl.when(f == g)
        def _():
            pr[...] = r[...] * wm[8 + g]

    @pl.when((f == 4) | (f == 5))
    def _():
        pr[...] = jnp.zeros(pr.shape, F32)

    @pl.when(f >= 6)
    def _():
        pr[...] = yp[...]

    w = wm[f]
    for k in range(4):
        image = y[k] - pr[k]
        if chained:
            image = image + coef[1:2, :] * img_in[k]
        fix = dot(bcat[k], acat[...])
        if first:
            new = image - fix
        else:
            new = u[k] - coef[0:1, :] * (image - fix)
        b = slot[4 * f + k]
        if last:
            direction = u[k] + coef[1:2, :] * d_in[k]
            lam_out[b] = lam_in[k] + coef[0:1, :] * direction
            u_out[b] = new
        else:
            u_out[k] = new
            xb[b] = new.astype(BF16)
            weighted = new * w
            sums[0:8, :] += jnp.sum((weighted * new).reshape(16, 8, BLK), axis=0)
            if not first:
                img_out[k] = image
                sums[8:16, :] += jnp.sum((weighted * image).reshape(16, 8, BLK), axis=0)

    if not last:

        @pl.when(f == pl.num_programs(0) - 1)
        def _():
            part[...] = jnp.zeros(part.shape, F32)
            part[0:1, :] = jnp.sum(sums[0:8, :], axis=0, keepdims=True)
            part[1:2, :] = jnp.sum(sums[8:16, :], axis=0, keepdims=True)


def update(kind, slot, tab, wm, h, c2, received, y, bcat, u=None, chain=None, closing=None):
    first, last, chained = kind == 0, kind == ITERS, kind >= 2
    face = pl.BlockSpec((4, BLK, BLK), lambda f, *_: (f, 0, 0))
    if first:
        received = [hbm(x) for x in received]
    args = [h, c2, *received, y, y, bcat]
    specs = [held(x.shape) for x in args[:6]]
    specs += [
        face,
        pl.BlockSpec((4, BLK, BLK), lambda f, *_: (jnp.where(f >= 6, 13 - f, 7), 0, 0)),
        pl.BlockSpec((4, BLK, 256), lambda f, *_: (f, 0, 0)),
    ]
    if not first:
        args.append(u)
        specs.append(face)
    if chained:
        args += list(chain)
        specs += [face, held(chain[1].shape), held(chain[2].shape)]
    vector, small = shape((32, BLK, BLK)), shape((8, BLK))
    if last:
        args += list(closing)
        specs += [face, face]
        outs, out_specs = [vector, vector], [whole(vector.shape)] * 2
    else:
        outs = [vector, shape((32, BLK, BLK), BF16), small]
        out_specs = [face, whole(vector.shape), whole(small.shape)]
        if not first:
            outs += [vector, shape((ROWS, BLK)), small]
            out_specs += [face, whole((ROWS, BLK)), whole(small.shape)]
    return pl.pallas_call(
        lambda *refs: update_body(kind, *refs),
        grid_spec=pltpu.PrefetchScalarGridSpec(
            num_scalar_prefetch=3,
            grid=(8,),
            in_specs=specs,
            out_specs=out_specs,
            scratch_shapes=[
                pltpu.VMEM((c2.shape[1], BLK), F32),
                pltpu.VMEM((256, BLK), BF16),
                pltpu.VMEM((4, BLK, BLK), F32),
                pltpu.VMEM((8, BLK), F32),
                pltpu.VMEM((16, BLK), F32),
            ],
        ),
        out_shape=outs,
        compiler_params=params(16),
        name=f"update_{kind}",
    )(slot, tab, wm, *args)


def on_device(dual_operators, local_loads, modes, coarse_matrix, coarse_loads, slot_block):
    n_sub, n_cluster = lax.axis_size("sub"), lax.axis_size("cluster")
    own, cluster = lax.axis_index("sub"), lax.axis_index("cluster")
    slot = slot_block[0]
    positions = jnp.arange(32, dtype=jnp.int32)
    inv = jnp.sum(positions[:, None] * (slot[:, None] == positions[None, :]).astype(jnp.int32), axis=0)
    there = jnp.stack([own > 0, own < n_sub - 1, cluster > 0, cluster < n_cluster - 1])
    one = jnp.ones((4,), F32)
    wm = jnp.concatenate([jnp.where(there, 0.5, 1.0), jnp.array([1.0, 1.0, 0.5, 0.5]), there.astype(F32), one]).astype(F32)

    device = jnp.arange(n_sub * n_cluster, dtype=jnp.int32)
    dz, dsub = device // n_sub, device % n_sub
    far = lambda now, mine: (now - mine) % 4
    tab = (
        (((dsub % 2) ^ (own % 2)) * 4 + far(dsub // 2 % 4, own // 2 % 4)) * 4 + far(dsub // 8, own // 8)
    ) * 4 + far(dz, cluster)

    def along_sub(value, source):
        return lax.ppermute(value, "sub", [(source(i), i) for i in range(n_sub)])

    def along_cluster(value, k):
        return lax.ppermute(value, "cluster", [((i + k) % n_cluster, i) for i in range(n_cluster)])

    def exchange(p0, p1, p2, p3):
        return [
            along_sub(p1, lambda i: (i - 1) % n_sub),
            along_sub(p0, lambda i: (i + 1) % n_sub),
            along_cluster(p3, -1),
            along_cluster(p2, 1),
        ]

    def gather(faces, groups):
        eo, el, er, ed, eu = groups
        mine = eo + along_sub(er, lambda i: (i - 1) % n_sub) + along_sub(el, lambda i: (i + 1) % n_sub)
        sent = lax.optimization_barrier(jnp.concatenate([mine, ed, eu], axis=0))
        z = [sent] + [along_cluster(sent, k) for k in (1, 2, 3)]
        mine, faces = lax.optimization_barrier((mine, faces))
        received = exchange(*faces)
        h = [z[k][:GRP] + z[(k + 1) % 4][GRP : 2 * GRP] + z[(k + 3) % 4][2 * GRP :] for k in range(4)]
        h = lax.optimization_barrier(jnp.concatenate(h, axis=0))
        for step in (8, 2):
            place = lambda i, k: i - i % (4 * step) + (i + k * step) % (4 * step)
            h = [h] + [along_sub(h, lambda i, k=k: place(i, k)) for k in (1, 2, 3)]
            h = jnp.concatenate(h, axis=0)
            h, received = lax.optimization_barrier((h, received))
        h = jnp.concatenate([h, along_sub(h, lambda i: i ^ 1)], axis=0)
        return h.reshape(128, GRP, BLK), received

    rs, *payload = prep(slot, modes, coarse_matrix)
    neighbours = exchange(*payload)
    bcat, bt2, c2, lam, xb = initial(slot, wm, rs, neighbours, coarse_matrix, coarse_loads)

    y, *sent = apply_dual(inv, dual_operators, xb, bt2, loads=local_loads, stream=True)
    h, received = gather(sent[:4], sent[4:])
    u, xb, part = update(0, slot, tab, wm, h, c2, received, y, bcat)
    chain, direction = None, None
    for kind in range(1, ITERS + 1):
        y, *sent = apply_dual(inv, dual_operators, xb, bt2, u=u, part=part, stream=kind == 1)
        h, received = gather(sent[:4], sent[4:])
        closing = (lam, direction) if kind == ITERS else None
        outs = update(kind, slot, tab, wm, h, c2, received, y, bcat, u, chain, closing)
        if kind < ITERS:
            new, xb, part, image, a, scal = outs
            direction = u if direction is None else u + scal[3] * direction
            lam = lam + scal[2] * direction
            u, chain = new, (image, a, scal)
    shape_out = local_loads.shape
    return outs[0].reshape(shape_out), outs[1].reshape(shape_out)


def solution(mesh):
    spec = P(("cluster", "sub"), None, None)
    flat = P(("cluster", "sub"), None)
    return jax.shard_map(
        on_device,
        mesh=mesh,
        in_specs=(spec, spec, spec, flat, P(), flat),
        out_specs=(spec, spec),
        check_vma=False,
    )
```
